32 devices in a mesh: ctx: 8 (over y, x, core), head: 4 (over z).
Axes of the slice: x: 2, y: 2, z: 4, core: 2. Of those that a mesh axis runs over, the one named last changes fastest.
Arguments:
- query_input: bfloat16 [8, 512, 4096], P('ctx', 'head'), may hold values from -6 to 6
- key_input: bfloat16 [8, 512, 512], P('ctx', 'head'), may hold values from -6 to 6
- value_input: bfloat16 [8, 512, 512], P('ctx', 'head'), may hold values from -6 to 6
- grad_input: bfloat16 [8, 512, 4096], P('ctx', 'head'), may hold values from -6 to 6
Outputs:
- attended: bfloat16 [8, 512, 4096], P('ctx', 'head')
- query_grad: float32 [8, 512, 4096], P('ctx', 'head')
- key_grad: float32 [8, 512, 512], P('ctx', 'head')
- value_grad: float32 [8, 512, 512], P('ctx', 'head')
The draws below stay inside these ranges and needn't reach their ends.
All inputs are finite; a program needn't handle non-finite values.
Results may differ from the reference program's by a relative error of at most 0.0076.
Values may be sent and summed in bfloat16 or wider, within the bound.
A program may use at most 192 MiB of HBM per device.

```python
import math
import jax
import jax.numpy as jnp
from jax import lax

HD = 128
HEADS = 32
KV_HEADS = 4
STRETCH = 256
BATCH = 2
SEQ = 2048
N_CTX = 8


def block_layout(tensor):
    columns = tensor.shape[-1]
    block_count = SEQ // STRETCH
    return tensor.reshape(BATCH, block_count, STRETCH, columns).transpose(1, 0, 2, 3).reshape(block_count, BATCH * STRETCH, columns)


def draw_query_input(key, part):
    full_shape = (BATCH, SEQ, HEADS, HD)
    base_key = jax.random.fold_in(key, 11)
    sample = jax.random.truncated_normal(base_key, -6.0, 6.0, full_shape, jnp.float32)
    return block_layout(sample.reshape(BATCH, SEQ, HEADS * HD)).astype(jnp.bfloat16)


def draw_key_input(key, part):
    full_shape = (BATCH, SEQ, KV_HEADS, HD)
    base_key = jax.random.fold_in(key, 13)
    sample = jax.random.truncated_normal(base_key, -6.0, 6.0, full_shape, jnp.float32)
    return block_layout(sample.reshape(BATCH, SEQ, KV_HEADS * HD)).astype(jnp.bfloat16)


def block_levels(rng, dims, cuts, low, high):
    level = 1.0
    for dim, parts in cuts:
        steps = jax.random.uniform(jax.random.fold_in(jax.random.fold_in(rng, 6), dim), (parts,), jnp.float32, low / len(cuts), high / len(cuts))
        level = level * jnp.repeat(jnp.exp(steps), dims[dim] // parts).reshape((-1,) + (1,) * (len(dims) - 1 - dim))
    return level


def centred(own_key, extent, spread, most, pieces=(), held_as=jnp.bfloat16):
    drawn = spread * jax.random.normal(own_key, extent, jnp.float32)
    if pieces:
        drawn = drawn * block_levels(own_key, extent, pieces, -0.22, 0.18)
    return jnp.clip(drawn, -most, most).astype(held_as)


def setup_inputs(seed: int = 0) -> dict:
    splits = jax.random.split(jax.random.key(seed), 5)
    return {
        "query_input": draw_query_input(jax.random.fold_in(splits[4], 71), 0),
        "key_input": draw_key_input(jax.random.fold_in(splits[4], 71), 0),
        "value_input": centred(splits[2], (N_CTX, BATCH * STRETCH, KV_HEADS * HD), 1.0, 6.0, ((0, 8), (1, 4))),
        "grad_input": centred(splits[3], (N_CTX, BATCH * STRETCH, HEADS * HD), 1.0, 6.0, ((0, 8), (1, 4))),
    }


def rounded(tensor):
    return lax.optimization_barrier(tensor.astype(jnp.bfloat16)).astype(jnp.float32)

def reference(query_input, key_input, value_input, grad_input):
    sharing = HEADS // KV_HEADS
    scaling = 1.0 / math.sqrt(HD)

    def to_sequences(tensor):
        columns = tensor.shape[-1]
        return tensor.reshape(N_CTX, BATCH, STRETCH, columns).transpose(1, 0, 2, 3).reshape(BATCH, SEQ, columns)

    def to_blocks(tensor):
        columns = tensor.shape[-1]
        return tensor.reshape(BATCH, N_CTX, STRETCH, columns).transpose(1, 0, 2, 3).reshape(N_CTX, BATCH * STRETCH, columns)

    def split_queries(tensor):
        return to_sequences(tensor).reshape(BATCH, SEQ, KV_HEADS, sharing, HD).transpose(0, 2, 3, 1, 4).reshape(BATCH * KV_HEADS, sharing, SEQ, HD)

    def split_pairs(tensor):
        return to_sequences(tensor).reshape(BATCH, SEQ, KV_HEADS, HD).transpose(0, 2, 1, 3).reshape(BATCH * KV_HEADS, SEQ, HD)
    positions = jnp.arange(SEQ, dtype=jnp.int32)
    causal = positions[None, :] <= positions[:, None]

    def single(operands):
        query_part = operands[0].astype(jnp.float32)
        key_part = operands[1].astype(jnp.float32)
        value_part = operands[2].astype(jnp.float32)
        grad_part = operands[3].astype(jnp.float32)
        raw_scores = jnp.einsum('gid,jd->gij', query_part, key_part) * scaling
        scores = jnp.where(causal[None], raw_scores, -jnp.inf)
        highest = lax.optimization_barrier(jnp.max(scores, axis=-1, keepdims=True))
        log_total = highest + jnp.log(lax.optimization_barrier(jnp.sum(jnp.exp(scores - highest), axis=-1, keepdims=True)))
        probs = jnp.exp(scores - log_total)
        weights = rounded(probs)
        attended = jnp.einsum('gij,jd->gid', weights, value_part).astype(jnp.bfloat16)
        attended_back = lax.optimization_barrier(attended).astype(jnp.float32)
        row_dot = lax.optimization_barrier(jnp.sum(grad_part * attended_back, axis=-1, keepdims=True))
        weight_grad = jnp.einsum('gid,jd->gij', grad_part, value_part)
        score_grad = rounded(probs * (weight_grad - row_dot))
        query_grad = scaling * jnp.einsum('gij,jd->gid', score_grad, key_part)
        key_grad = scaling * jnp.einsum('gij,gid->jd', score_grad, query_part)
        value_grad = jnp.einsum('gij,gid->jd', weights, grad_part)
        return (attended, query_grad, key_grad, value_grad)
    attended, query_grad, key_grad, value_grad = lax.map(single, (split_queries(query_input), split_pairs(key_input), split_pairs(value_input), split_queries(grad_input)))

    def merge_queries(tensor):
        return to_blocks(tensor.reshape(BATCH, KV_HEADS, sharing, SEQ, HD).transpose(0, 3, 1, 2, 4).reshape(BATCH, SEQ, HEADS * HD))

    def merge_pairs(tensor):
        return to_blocks(tensor.reshape(BATCH, KV_HEADS, SEQ, HD).transpose(0, 2, 1, 3).reshape(BATCH, SEQ, KV_HEADS * HD))
    return (merge_queries(attended), merge_queries(query_grad), merge_pairs(key_grad), merge_pairs(value_grad))
```

```python
import functools
import math

import jax
import jax.numpy as jnp
from jax import lax
from jax.experimental import pallas as pl
from jax.experimental.pallas import tpu as pltpu
from jax.sharding import PartitionSpec as P

HD = 128
NT = (((1,), (1,)), ((), ()))
TN = (((0,), (0,)), ((), ()))
F32 = jnp.float32
BF16 = jnp.bfloat16


def dot(a, b, dims=(((1,), (0,)), ((), ()))):
    return lax.dot_general(a, b, dims, preferred_element_type=F32)


def attend_kernel(rows, sharing, q_ref, g_ref, k_ref, v_ref, o_ref, dq_ref, dk_ref, dv_ref,
                  s_scr, p_scr, qs, gs, qn, gn, acc, top, total, drow):
    block = lax.axis_index("ctx")
    half = lax.axis_index("head") % 2
    span = 2 * rows
    wide = rows * sharing
    step_cols = 2 * rows
    scaling = 1.0 / math.sqrt(HD)
    factor = scaling * math.log2(math.e)
    for h in range(sharing):
        qs[h * rows:(h + 1) * rows, :] = q_ref[:, h * HD:(h + 1) * HD]
        gs[h * rows:(h + 1) * rows, :] = g_ref[:, h * HD:(h + 1) * HD]
    dk_ref[...] = jnp.zeros_like(dk_ref)
    dv_ref[...] = jnp.zeros_like(dv_ref)

    def keys_at(b):
        return pl.ds(pl.multiple_of(b * span, span), span)

    top[...] = jnp.full_like(top, -jnp.inf)

    def scores(b, masked):
        kb = k_ref[keys_at(b), :]
        for c in range(0, wide, step_cols):
            cols = slice(c, c + step_cols)
            s = dot(kb, qs[cols, :], NT)
            if masked:
                key_pos = lax.broadcasted_iota(jnp.int32, s.shape, 0)
                row_pos = half * rows + lax.broadcasted_iota(jnp.int32, s.shape, 1) % rows
                s = jnp.where(key_pos <= row_pos, s, -jnp.inf)
            s_scr[keys_at(b), cols] = s
            top[:, cols] = jnp.maximum(top[:, cols], s.reshape(span // 8, 8, step_cols).max(axis=0))

    @pl.loop(0, block)
    def _(b):
        scores(b, False)

    scores(block, True)
    highest = jnp.max(top[...], axis=0, keepdims=True) * factor
    total[...] = jnp.zeros_like(total)
    acc[...] = jnp.zeros_like(acc)

    @pl.loop(0, block + 1)
    def _(b):
        vb = v_ref[keys_at(b), :]
        for c in range(0, wide, step_cols):
            cols = slice(c, c + step_cols)
            p = jnp.exp2(s_scr[keys_at(b), cols] * factor - highest[:, cols])
            total[:, cols] += p.reshape(span // 8, 8, step_cols).sum(axis=0)
            pb = p.astype(BF16)
            p_scr[keys_at(b), cols] = pb
            acc[cols, :] += dot(pb, vb, TN)

    inverse = 1.0 / jnp.sum(total[...], axis=0, keepdims=True)
    turned = []
    for h in range(sharing):
        part = slice(h * rows, (h + 1) * rows)
        inv = jnp.broadcast_to(inverse[:, part], (HD, rows)).T
        turned.append(inv)
        out = (acc[part, :] * inv).astype(BF16)
        o_ref[:, h * HD:(h + 1) * HD] = out
        g = gs[part, :].astype(F32)
        drow[:, part] = jnp.sum((g * out.astype(F32)).T, axis=0, keepdims=True)
        gn[part, :] = (g * inv).astype(BF16)
        qn[part, :] = (qs[part, :].astype(F32) * (inv * scaling)).astype(BF16)
    acc[...] = jnp.zeros_like(acc)

    @pl.loop(0, block + 1)
    def _(b):
        kb = k_ref[keys_at(b), :]
        vb = v_ref[keys_at(b), :]
        dk = jnp.zeros((span, HD), F32)
        dv = jnp.zeros((span, HD), F32)
        for c in range(0, wide, step_cols):
            cols = slice(c, c + step_cols)
            dp = dot(vb, gs[cols, :], NT)
            pb = p_scr[keys_at(b), cols]
            ds = (pb.astype(F32) * (dp - drow[:, cols])).astype(BF16)
            dk += dot(ds, qn[cols, :])
            dv += dot(pb, gn[cols, :])
            acc[cols, :] += dot(ds, kb, TN)
        dk_ref[keys_at(b), :] = dk.astype(dk_ref.dtype)
        dv_ref[keys_at(b), :] = dv.astype(dv_ref.dtype)

    for h in range(sharing):
        part = slice(h * rows, (h + 1) * rows)
        inv = jnp.broadcast_to(inverse[:, part], (HD, rows)).T
        dq_ref[:, h * HD:(h + 1) * HD] = acc[part, :] * (inv * scaling)


def attend(q, g, k_all, v_all):
    rows, width = q.shape
    seq, pair_width = k_all.shape
    pairs = pair_width // HD
    sharing = width // pair_width
    wide = rows * sharing
    by_head = lambda r, w: pl.BlockSpec((r, w), lambda i: (0, i))
    return pl.pallas_call(
        functools.partial(attend_kernel, rows, sharing),
        grid=(pairs,),
        out_shape=(
            jax.ShapeDtypeStruct((rows, width), BF16),
            jax.ShapeDtypeStruct((rows, width), F32),
            jax.ShapeDtypeStruct((seq, pair_width), F32),
            jax.ShapeDtypeStruct((seq, pair_width), F32),
        ),
        in_specs=[by_head(rows, sharing * HD)] * 2 + [by_head(seq, HD)] * 2,
        out_specs=(by_head(rows, sharing * HD), by_head(rows, sharing * HD), by_head(seq, HD), by_head(seq, HD)),
        scratch_shapes=[
            pltpu.VMEM((seq, wide), F32),
            pltpu.VMEM((seq, wide), BF16),
            pltpu.VMEM((wide, HD), BF16),
            pltpu.VMEM((wide, HD), BF16),
            pltpu.VMEM((wide, HD), BF16),
            pltpu.VMEM((wide, HD), BF16),
            pltpu.VMEM((wide, HD), F32),
            pltpu.VMEM((8, wide), F32),
            pltpu.VMEM((8, wide), F32),
            pltpu.VMEM((1, wide), F32),
        ],
        compiler_params=pltpu.CompilerParams(vmem_limit_bytes=60 * 1024 * 1024),
        name="attend",
    )(q, g, k_all, v_all)


def from_partner(value):
    pairs = [(source, source ^ 1) for source in range(lax.axis_size("head"))]
    return lax.ppermute(value, "head", pairs)


def on_device(query_input, key_input, value_input, grad_input):
    rows = query_input.shape[1]
    pair_width = key_input.shape[2]
    blocks = lax.axis_size("ctx")
    half = lax.axis_index("head") % 2
    own = jnp.concatenate([key_input[0], value_input[0]], axis=1)
    other = from_partner(own)
    both = jnp.where(half == 0, jnp.concatenate([own, other], axis=0), jnp.concatenate([other, own], axis=0))
    gathered = lax.all_gather(both, "ctx", axis=0, tiled=True)
    attended, query_grad, dk, dv = attend(
        query_input[0], grad_input[0], gathered[:, :pair_width], gathered[:, pair_width:]
    )
    sums = jnp.concatenate([dk, dv], axis=1)
    sums = lax.psum_scatter(sums, "ctx", scatter_dimension=0, tiled=True)
    outgoing = lax.dynamic_slice_in_dim(sums, (1 - half) * rows, rows, 0).astype(BF16)
    mine = lax.dynamic_slice_in_dim(sums, half * rows, rows, 0) + from_partner(outgoing).astype(F32)
    return (attended[None], query_grad[None], mine[None, :, :pair_width], mine[None, :, pair_width:])


def solution(mesh):
    spec = P("ctx", "head", None)
    return jax.shard_map(on_device, mesh=mesh, in_specs=(spec,) * 4, out_specs=(spec,) * 4, check_vma=False)
```

```python
import functools
import math

import jax
import jax.numpy as jnp
from jax import lax
from jax.experimental import pallas as pl
from jax.experimental.pallas import tpu as pltpu
from jax.sharding import PartitionSpec as P

HD = 128
NT = (((1,), (1,)), ((), ()))
TN = (((0,), (0,)), ((), ()))
F32 = jnp.float32
BF16 = jnp.bfloat16


def dot(a, b, dims=(((1,), (0,)), ((), ()))):
    return lax.dot_general(a, b, dims, preferred_element_type=F32)


MESH = pl.DeviceIdType.MESH


def pieces_of(rows):
    unit = 16
    units = rows // unit
    count = min(3, units)
    sizes = [(units // count + (1 if i < units % count else 0)) * unit for i in range(count)]
    starts = [sum(sizes[:i]) for i in range(count)]
    return [slice(a, a + s) for a, s in zip(starts, sizes)]


def orders_of(bits, count):
    links = [d for d in range(bits + 1) if d != bits - 1]
    return [[links[(i + p) % len(links)] for i in range(len(links))] for p in range(count)]


def my_bits(bits):
    block = lax.axis_index("ctx")
    return [block // 2 ** (bits - 1 - d) % 2 for d in range(bits)] + [lax.axis_index("head") % 2]


def partner_of(bits, me, d):
    if d == bits:
        return {"head": lax.axis_index("head") + 1 - 2 * me[d]}
    return {"ctx": lax.axis_index("ctx") + (1 - 2 * me[d]) * 2 ** (bits - 1 - d)}


def mirror_of(bits):
    return {"ctx": 2 ** bits - 1 - lax.axis_index("ctx")}


def greet(bits, me):
    barrier = pltpu.get_barrier_semaphore()
    for d in range(bits + 1):
        pl.semaphore_signal(barrier, inc=1, device_id=partner_of(bits, me, d), device_id_type=MESH)
    pl.semaphore_signal(barrier, inc=1, device_id=mirror_of(bits), device_id_type=MESH)
    pl.semaphore_wait(barrier, bits + 2)


def gather_steps(bits, me, arrays, heads, parts, sems):
    link_send, link_recv, core_send, core_recv = sems
    orders = orders_of(bits, len(parts))
    regions = [list(me) for _ in parts]
    fresh = [list(me) for _ in parts]
    links, cores = [], []

    def copy(ref, index, d, send, recv):
        return pltpu.make_async_remote_copy(
            src_ref=ref.at[index], dst_ref=ref.at[index], send_sem=send, recv_sem=recv,
            device_id=partner_of(bits, me, d), device_id_type=MESH)

    def step(k):
        for c in links:
            c.wait()
        links.clear()
        for p in range(len(parts)):
            if 0 < k <= bits:
                d = orders[p][k - 1]
                fresh[p] = list(regions[p])
                fresh[p][d] = 1 - me[d]
                regions[p][d] = slice(None)
        for p, part in enumerate(parts):
            for a, ref in enumerate(arrays):
                if k < bits:
                    c = copy(ref, (heads, *regions[p], part), orders[p][k], link_send.at[p, k, a], link_recv.at[p, k, a])
                    c.start()
                    links.append(c)
        for p, part in enumerate(parts):
            for a, ref in enumerate(arrays):
                if k <= bits:
                    c = copy(ref, (heads, *fresh[p], part), bits - 1, core_send.at[p, k, a], core_recv.at[p, k, a])
                    c.start()
                    cores.append(c)
        if k > bits:
            for c in cores:
                c.wait()

    return [functools.partial(step, k) for k in range(bits + 2)]


def scatter_steps(bits, me, arrays, outs, h, parts, held, send_sem, recv_sem):
    orders = [[bits - 1] + order[::-1] for order in orders_of(bits, len(parts))]
    now = [[(ref, (part,)) for ref in arrays] for part in parts]
    dims = [list(range(bits + 1)) for _ in parts]
    copies = []

    def pick(p, d, value, tail):
        return (h, *(value if e == d else slice(None) for e in dims[p]), *tail)

    def step(k):
        if k > 0:
            for p, part in enumerate(parts):
                d = orders[p][k - 1]
                for a in range(2):
                    copies[2 * p + a].wait()
                    ref, tail = now[p][a]
                    slot = held[p][k - 1][a]
                    sums = ref[pick(p, d, me[d], tail)].astype(F32) + slot[h].astype(F32)
                    if k > bits:
                        outs[a][part, h * HD:(h + 1) * HD] = sums
                    else:
                        slot[h] = sums.astype(slot.dtype)
                    now[p][a] = (slot, (slice(None),))
                dims[p].remove(d)
            copies.clear()
        if k <= bits:
            for p in range(len(parts)):
                d = orders[p][k]
                for a in range(2):
                    ref, tail = now[p][a]
                    c = pltpu.make_async_remote_copy(
                        src_ref=ref.at[pick(p, d, 1 - me[d], tail)], dst_ref=held[p][k][a].at[h],
                        send_sem=send_sem.at[p, k, a], recv_sem=recv_sem.at[p, k, a],
                        device_id=partner_of(bits, me, d), device_id_type=MESH)
                    c.start()
                    copies.append(c)

    return [functools.partial(step, k) for k in range(bits + 2)]


def layer_kernel(bits, sharing, q_ref, g_ref, k_ref, v_ref, o_ref, dq_ref, ok_ref, ov_ref,
                 ka, va, dka, dva, s_scr, p_scr, qs, gs, qn, gn, acc, top, total, drow,
                 qm, gm, om, dm, oin, din, swap_send, swap_recv,
                 own_sem, link_send, link_recv, core_send, core_recv, send_sem, recv_sem, *slots):
    rows, pair_width = k_ref.shape
    pairs = pair_width // HD
    block = lax.axis_index("ctx")
    half = lax.axis_index("head") % 2
    span = 2 * rows
    wide = rows * sharing
    step_cols = 2 * rows
    scaling = 1.0 / math.sqrt(HD)
    factor = scaling * math.log2(math.e)
    me = my_bits(bits)
    parts = pieces_of(rows)
    slot_list = iter(slots)
    held = [[[next(slot_list) for _ in range(2)] for _ in range(bits + 1)] for _ in parts]

    greet(bits, me)
    own = [pltpu.make_async_copy(src.at[:, h * HD:(h + 1) * HD], dst.at[(h, *me)], own_sem.at[h, a])
           for h in range(pairs) for a, (src, dst) in enumerate(((k_ref, ka), (v_ref, va)))]
    for c in own:
        c.start()
    for c in own:
        c.wait()
    groups = [slice(0, 1)] + ([slice(1, pairs)] if pairs > 1 else [])
    gathers = [gather_steps(bits, me, (ka, va), heads, parts,
                            [r.at[i] for r in (link_send, link_recv, core_send, core_recv)])
               for i, heads in enumerate(groups)]
    pending = []

    def advance(count=1):
        for work in pending:
            for _ in range(count):
                if work:
                    work.pop(0)()
        pending[:] = [work for work in pending if work]

    def drain(work):
        while work:
            work.pop(0)()

    def keys_at(b):
        return pl.ds(pl.multiple_of(b * span, span), span)

    def bits_of(b):
        return tuple(b // 2 ** (bits - 1 - d) % 2 for d in range(bits))

    def first_gather_ready():
        drain(gathers[0])
        if len(gathers) > 1:
            gathers[1].pop(0)()

    count = 2 ** bits
    light = block < count // 2
    last = pairs - 1
    last_base = last * sharing * HD
    last_cols = slice(last_base, last_base + sharing * HD)

    def swap(i, src, dst):
        return pltpu.make_async_remote_copy(
            src_ref=src, dst_ref=dst, send_sem=swap_send.at[i], recv_sem=swap_recv.at[i],
            device_id=mirror_of(bits), device_id_type=MESH)

    lend = [swap(0, q_ref.at[:, last_cols], qm), swap(1, g_ref.at[:, last_cols], gm)]
    give = [swap(2, om, oin), swap(3, dm, din)]

    def clear(g, first):
        for ref in (dka, dva):
            @pl.loop(first, count)
            def _(b):
                ref[(g, *bits_of(b))] = jnp.zeros((2, rows, HD), ref.dtype)

    def attend_head(g, q_src, g_src, base, block, out_ref, out_base, dq_out, again, polled):
        for h in range(sharing):
            qs[h * rows:(h + 1) * rows, :] = q_src[:, base + h * HD:base + (h + 1) * HD]
            gs[h * rows:(h + 1) * rows, :] = g_src[:, base + h * HD:base + (h + 1) * HD]

        if not again:
            clear(g, block + 1)
        top[...] = jnp.full_like(top, -jnp.inf)
        if g == 0:
            first_gather_ready()
        if g == 1:
            drain(gathers[1])

        def load(ref, b):
            return ref[(g, *bits_of(b))].reshape(span, HD)

        def scores(b, masked):
            kb = load(ka, b)
            for c in range(0, wide, step_cols):
                cols = slice(c, c + step_cols)
                s = dot(kb, qs[cols, :], NT)
                if masked:
                    key_pos = lax.broadcasted_iota(jnp.int32, s.shape, 0)
                    row_pos = half * rows + lax.broadcasted_iota(jnp.int32, s.shape, 1) % rows
                    s = jnp.where(key_pos <= row_pos, s, -jnp.inf)
                s_scr[keys_at(b), cols] = s
                top[:, cols] = jnp.maximum(top[:, cols], s.reshape(span // 8, 8, step_cols).max(axis=0))

        @pl.loop(0, block)
        def _(b):
            scores(b, False)

        scores(block, True)
        polled()
        highest = jnp.max(top[...], axis=0, keepdims=True) * factor
        total[...] = jnp.zeros_like(total)
        acc[...] = jnp.zeros_like(acc)

        @pl.loop(0, block + 1)
        def _(b):
            vb = load(va, b)
            for c in range(0, wide, step_cols):
                cols = slice(c, c + step_cols)
                p = jnp.exp2(s_scr[keys_at(b), cols] * factor - highest[:, cols])
                total[:, cols] += p.reshape(span // 8, 8, step_cols).sum(axis=0)
                pb = p.astype(BF16)
                p_scr[keys_at(b), cols] = pb
                acc[cols, :] += dot(pb, vb, TN)

        polled()
        inverse = 1.0 / jnp.sum(total[...], axis=0, keepdims=True)
        for h in range(sharing):
            part = slice(h * rows, (h + 1) * rows)
            inv = jnp.broadcast_to(inverse[:, part], (HD, rows)).T
            out = (acc[part, :] * inv).astype(BF16)
            out_ref[:, out_base + h * HD:out_base + (h + 1) * HD] = out
            grad = gs[part, :].astype(F32)
            drow[:, part] = jnp.sum((grad * out.astype(F32)).T, axis=0, keepdims=True)
            gn[part, :] = (grad * inv).astype(BF16)
            qn[part, :] = (qs[part, :].astype(F32) * (inv * scaling)).astype(BF16)
        acc[...] = jnp.zeros_like(acc)

        @pl.loop(0, block + 1)
        def _(b):
            kb = load(ka, b)
            vb = load(va, b)
            dk = jnp.zeros((span, HD), F32)
            dv = jnp.zeros((span, HD), F32)
            for c in range(0, wide, step_cols):
                cols = slice(c, c + step_cols)
                dp = dot(vb, gs[cols, :], NT)
                pb = p_scr[keys_at(b), cols]
                ds = (pb.astype(F32) * (dp - drow[:, cols])).astype(BF16)
                dk += dot(ds, qn[cols, :])
                dv += dot(pb, gn[cols, :])
                acc[cols, :] += dot(ds, kb, TN)
            for ref, add in ((dka, dk), (dva, dv)):
                if again:
                    add = add + load(ref, b).astype(F32)
                ref[(g, *bits_of(b))] = add.astype(ref.dtype).reshape(2, rows, HD)

        for h in range(sharing):
            part = slice(h * rows, (h + 1) * rows)
            inv = jnp.broadcast_to(inverse[:, part], (HD, rows)).T
            dq_out[:, out_base + h * HD:out_base + (h + 1) * HD] = (acc[part, :] * (inv * scaling)).astype(dq_out.dtype)

    for g in range(last):
        polls = []

        def polled():
            if g == 0:
                gathers[1].pop(0)()
                if polls:
                    @pl.when(~light)
                    def _():
                        for c in lend:
                            c.start()
                polls.append(1)
            advance()

        base = g * sharing * HD
        attend_head(g, q_ref, g_ref, base, block, o_ref, base, dq_ref, False, polled)
        advance()
        work = scatter_steps(bits, me, (dka, dva), (ok_ref, ov_ref), g, parts, held, send_sem.at[g], recv_sem.at[g])
        work.pop(0)()
        pending.append(work)

    @pl.when(light)
    def _():
        nothing = lambda: None
        attend_head(last, q_ref, g_ref, last_base, block, o_ref, last_base, dq_ref, False, nothing)
        for c in lend:
            c.wait_recv()
        attend_head(last, qm, gm, 0, count - 1 - block, om, 0, dm, True, nothing)
        for c in give:
            c.start()

    @pl.when(~light)
    def _():
        clear(last, 0)

    work = scatter_steps(bits, me, (dka, dva), (ok_ref, ov_ref), last, parts, held, send_sem.at[last], recv_sem.at[last])
    work.pop(0)()
    pending.append(work)
    while pending:
        advance()

    @pl.when(light)
    def _():
        for c in give:
            c.wait_send()

    @pl.when(~light)
    def _():
        for c in lend:
            c.wait_send()
        for c in give:
            c.wait_recv()
        o_ref[:, last_cols] = oin[...]
        dq_ref[:, last_cols] = din[...].astype(F32)


def layer(bits, q, g, k, v):
    rows, width = q.shape
    pair_width = k.shape[1]
    pairs = pair_width // HD
    sharing = width // pair_width
    wide = rows * sharing
    seq = 2 ** (bits + 1) * rows
    parts = pieces_of(rows)
    count = len(parts)
    vmem = pl.BlockSpec(memory_space=pltpu.VMEM)
    whole = pltpu.VMEM((pairs,) + (2,) * (bits + 1) + (rows, HD), BF16)
    sem = pltpu.SemaphoreType.DMA
    slots = [pltpu.VMEM((pairs,) + (2,) * (bits - k) + (part.stop - part.start, HD), BF16)
             for part in parts for k in range(bits + 1) for _ in range(2)]
    return pl.pallas_call(
        functools.partial(layer_kernel, bits, sharing),
        out_shape=(
            jax.ShapeDtypeStruct((rows, width), BF16),
            jax.ShapeDtypeStruct((rows, width), F32),
            jax.ShapeDtypeStruct((rows, pair_width), F32),
            jax.ShapeDtypeStruct((rows, pair_width), F32),
        ),
        in_specs=[vmem] * 4,
        out_specs=(vmem,) * 4,
        scratch_shapes=[
            whole, whole, whole, whole,
            pltpu.VMEM((seq, wide), F32),
            pltpu.VMEM((seq, wide), BF16),
            pltpu.VMEM((wide, HD), BF16),
            pltpu.VMEM((wide, HD), BF16),
            pltpu.VMEM((wide, HD), BF16),
            pltpu.VMEM((wide, HD), BF16),
            pltpu.VMEM((wide, HD), F32),
            pltpu.VMEM((8, wide), F32),
            pltpu.VMEM((8, wide), F32),
            pltpu.VMEM((1, wide), F32),
            *[pltpu.VMEM((rows, sharing * HD), BF16) for _ in range(6)],
            sem((4,)),
            sem((4,)),
            sem((pairs, 2)),
            sem((2, count, bits, 2)),
            sem((2, count, bits, 2)),
            sem((2, count, bits + 1, 2)),
            sem((2, count, bits + 1, 2)),
            sem((pairs, count, bits + 1, 2)),
            sem((pairs, count, bits + 1, 2)),
        ] + slots,
        compiler_params=pltpu.CompilerParams(collective_id=0, has_side_effects=True, vmem_limit_bytes=60 * 2**20),
        name="layer",
    )(q, g, k, v)


def on_device(query_input, key_input, value_input, grad_input):
    bits = (lax.axis_size("ctx") - 1).bit_length()
    outs = layer(bits, query_input[0], grad_input[0], key_input[0], value_input[0])
    return tuple(out[None] for out in outs)


def solution(mesh):
    spec = P("ctx", "head", None)
    return jax.shard_map(on_device, mesh=mesh, in_specs=(spec,) * 4, out_specs=(spec,) * 4, check_vma=False)
```
